32 devices in a mesh: prow: 4 (over y, x), pcol: 8 (over z, core).
Axes of the slice: x: 2, y: 2, z: 4, core: 2. Of those that a mesh axis runs over, the one named last changes fastest.
Arguments:
- inverse_block: bfloat16 [4096, 4096], P('prow', 'pcol'), as said below
- factor_cols: bfloat16 [4096, 2, 2048], P('prow', None, 'pcol'), may hold values from -6 to 6
- pattern: int32 [2, 32], replicated, may hold values from 0 to 1, as said below
Outputs:
- inverse_cols: bfloat16 [4096, 2, 2048], P(('pcol', 'prow'))
The draws below stay inside these ranges and needn't reach their ends.
Inputs may be any that keep to these rules, and one draw needn't show every extreme that they name: inverse_block is symmetric up to rounding. `pattern`: for each supernode, each aligned group of 8 row blocks holds 1 to 4 nonzero blocks, and some group holds exactly 4.
All inputs are finite; a program needn't handle non-finite values.
Results may differ from the reference program's by a relative error of at most 0.013.
Values may be sent and summed in bfloat16 or wider, within the bound.
No kernel may reach another device: no remote copies, remote signals or barrier semaphores. Data moves between devices by JAX's collectives and lax.ppermute only.
A program may use at most 64 MiB of HBM per device.

```python
import jax
import jax.numpy as jnp
from jax import lax

W = 2048
BLK = 128
NBP = 8
MAXB = 4
NBLK = 32
ROWS = 4096


def draw_inverse_block(key, part):
    noise = jax.random.normal(jax.random.fold_in(key, 11), (ROWS, ROWS), jnp.float32)
    symmetric = (noise + jnp.transpose(noise)) * (0.5 / ROWS ** 0.5)
    row_ids = jnp.arange(ROWS)
    symmetric = symmetric + 1.5 * (row_ids[:, None] == row_ids[None, :]).astype(jnp.float32)
    return symmetric.astype(jnp.bfloat16)


def draw_pattern(key, part):
    groups = NBLK // NBP
    key_count = jax.random.fold_in(key, 21)
    key_force = jax.random.fold_in(key, 22)
    key_order = jax.random.fold_in(key, 23)
    counts = jax.random.randint(key_count, (2, groups), 1, MAXB + 1)
    forced = jax.random.randint(key_force, (2,), 0, groups)
    counts = jnp.where(jnp.arange(groups)[None, :] == forced[:, None], MAXB, counts)
    scores = jax.random.randint(key_order, (2, groups, NBP), 0, 1 << 20) * NBP + jnp.arange(NBP)[None, None, :]
    ranks = jnp.argsort(jnp.argsort(scores, axis=2, stable=True), axis=2, stable=True)
    present = (ranks < counts[:, :, None]).astype(jnp.int32)
    return present.reshape(2, NBLK)


def steps_of(own_key, dims, cuts, low, high):
    factor_of, own = 1.0, jax.random.fold_in(own_key, 6)
    for axis_at, parts in cuts:
        steps = jnp.exp(jax.random.uniform(jax.random.fold_in(own, axis_at), (parts,), jnp.float32, low / len(cuts), high / len(cuts)))
        factor_of = factor_of * jnp.repeat(steps, dims[axis_at] // parts).reshape([-1 if axis == axis_at else 1 for axis in range(len(dims))])
    return factor_of


def bell_draw(stream_key, extent, scale, limit, pieces=(), kind=jnp.bfloat16):
    array = scale * jax.random.normal(stream_key, extent, jnp.float32)
    if pieces:
        array = array * steps_of(stream_key, extent, pieces, -0.22, 0.18)
    return jnp.clip(array, -limit, limit).astype(kind)


def setup_inputs(seed: int = 0) -> dict:
    arg_keys = jax.random.split(jax.random.key(seed), 4)
    return {
        "inverse_block": draw_inverse_block(jax.random.fold_in(arg_keys[3], 71), 0),
        "factor_cols": bell_draw(arg_keys[1], (ROWS, 2, W), 1.0, 6.0, ((0, 4), (2, 8))),
        "pattern": draw_pattern(jax.random.fold_in(arg_keys[3], 71), 0),
    }


def reference(inverse_block, factor_cols, pattern):
    row_mask = jnp.repeat(jnp.transpose(pattern), BLK, axis=0).astype(jnp.bfloat16)
    masked = factor_cols * row_mask[:, :, None]
    flat_rows = masked.reshape(ROWS, 2 * W)
    group_rows = NBP * BLK

    def add_group(total, group_id):
        begin_row = (group_id * group_rows).astype(jnp.int32)
        left_cols = lax.dynamic_slice_in_dim(inverse_block, begin_row, group_rows, 1)
        piece_rows = lax.dynamic_slice_in_dim(flat_rows, begin_row, group_rows, 0)
        partial_term = jnp.dot(left_cols, piece_rows, preferred_element_type=jnp.float32)
        return total + partial_term.astype(jnp.bfloat16).astype(jnp.float32), None

    start_total = jnp.zeros((ROWS, 2 * W), jnp.float32)
    total, unused = lax.scan(add_group, start_total, jnp.arange(NBLK // NBP, dtype=jnp.int32))
    return (-total).astype(jnp.bfloat16).reshape(ROWS, 2, W)
```

```python
import functools

import jax
import jax.numpy as jnp
from jax import lax
from jax.experimental import pallas as pl
from jax.experimental.pallas import tpu as pltpu
from jax.sharding import PartitionSpec as P

MAXB = 4
VMEM = pl.BlockSpec(memory_space=pltpu.VMEM)
SMEM = pl.BlockSpec(memory_space=pltpu.SMEM)


def swap(x, axis, mask):
    size = lax.axis_size(axis)
    return lax.ppermute(x, axis, [(i, i ^ mask) for i in range(size)])


def slots_of(pattern_ref, node, first, groups):
    ids = [jnp.int32(0)] * MAXB
    count = jnp.int32(0)
    for b in range(groups):
        present = pattern_ref[node, first + b]
        for k in range(MAXB):
            ids[k] = jnp.where((present == 1) & (count == k), b, ids[k])
        count = count + present
    return ids, count


def pack_factor_kernel(pattern_ref, factor_ref, out_ref, *, groups, rows):
    first = lax.axis_index("prow") * groups
    for node in range(2):
        ids, _ = slots_of(pattern_ref, node, first, groups)
        for k in range(MAXB):
            block = factor_ref[pl.ds(pl.multiple_of(ids[k] * rows, rows), rows), :, :]
            out_ref[node, k * rows : (k + 1) * rows, :] = block[:, node, :]


def pack_factor(pattern, factor, groups):
    rows = factor.shape[0] // groups
    shape = (2, MAXB * rows, factor.shape[2])
    return pl.pallas_call(
        functools.partial(pack_factor_kernel, groups=groups, rows=rows),
        out_shape=jax.ShapeDtypeStruct(shape, factor.dtype),
        in_specs=[SMEM, VMEM],
        out_specs=VMEM,
        name="pack_factor",
    )(pattern, factor)


def pack_left_kernel(pattern_ref, own_ref, other_ref, out_ref, *, groups, rows, owners):
    here = lax.axis_index("prow")
    piece = own_ref.shape[1] // owners
    for node in range(2):
        ids, count = slots_of(pattern_ref, node, here * groups, groups)
        for k in range(MAXB):
            block = pl.ds(pl.multiple_of(ids[k] * rows, rows), rows)
            for c, ref in enumerate((own_ref, other_ref)):
                turned = -ref[block, :].T
                turned = jnp.where(count > k, turned, jnp.zeros_like(turned))
                for owner in range(owners):
                    at = (jnp.bitwise_xor(here, owner) * 2 + c) * piece
                    out_ref[
                        node, pl.ds(pl.multiple_of(at, piece), piece), k * rows : (k + 1) * rows
                    ] = turned[owner * piece : (owner + 1) * piece]


def pack_left(pattern, own, other, groups, owners):
    rows = own.shape[0] // groups
    shape = (2, 2 * own.shape[1], MAXB * rows)
    return pl.pallas_call(
        functools.partial(pack_left_kernel, groups=groups, rows=rows, owners=owners),
        out_shape=jax.ShapeDtypeStruct(shape, own.dtype),
        in_specs=[SMEM, VMEM, VMEM],
        out_specs=VMEM,
        name="pack_left",
    )(pattern, own, other)


def unpack_kernel(*refs):
    out_ref = refs[-1]
    here = lax.axis_index("pcol")
    width = refs[0].shape[1]
    for u in range((len(refs) - 1) // 2):
        both = jnp.stack([refs[2 * u][...], refs[2 * u + 1][...]], axis=1)
        at = pl.multiple_of(jnp.bitwise_xor(here, u) * width, width)
        out_ref[:, :, pl.ds(at, width)] = both


def unpack(parts):
    rows, width = parts[0].shape
    if width % 128:
        slots = jnp.stack(parts).reshape(-1, 2, rows, width)
        order = jnp.bitwise_xor(lax.axis_index("pcol"), jnp.arange(len(slots)))
        return jnp.take(slots, order, axis=0).transpose(2, 1, 0, 3).reshape(rows, 2, -1)
    return pl.pallas_call(
        unpack_kernel,
        out_shape=jax.ShapeDtypeStruct((rows, 2, width * len(parts) // 2), parts[0].dtype),
        in_specs=[VMEM] * len(parts),
        out_specs=VMEM,
        name="unpack",
    )(*parts)


def reduce_rows(part, owners, bits):
    count = owners.bit_length() - 1
    acc = part.reshape((2,) * count + (part.shape[0] // owners, part.shape[1]))
    left = list(range(count))[::-1]
    for bit in bits:
        axis = left.index(bit)
        left.remove(bit)
        keep = lax.index_in_dim(acc, 0, axis, keepdims=False)
        give = lax.index_in_dim(acc, 1, axis, keepdims=False)
        got = swap(give, "prow", 1 << bit)
        acc = (keep.astype(jnp.float32) + got.astype(jnp.float32)).astype(part.dtype)
    return acc


def local(inverse_block, factor_cols, pattern):
    owners = lax.axis_size("prow")
    chips = lax.axis_size("pcol") // 2
    groups = pattern.shape[1] // owners
    packed = pack_factor(pattern, factor_cols, groups)
    held = {(0, node): packed[node] for node in range(2)}
    for node in range(2):
        for m in sorted(range(1, chips), key=lambda m: (bin(m).count("1"), -m)):
            low = m & -m
            held[m, node] = swap(held[m ^ low, node], "pcol", 2 * low)
    other = swap(inverse_block, "pcol", 1)
    left = pack_left(pattern, inverse_block, other, groups, owners)
    bits = list(range(owners.bit_length() - 1))
    parts = [None] * (4 * chips)
    for m in range(chips):
        for node in range(2):
            part = jnp.dot(left[node], held[m, node], preferred_element_type=jnp.float32)
            part = part.astype(jnp.bfloat16)
            turn = (m + node) % 2
            acc = reduce_rows(part, owners, bits if turn == 0 else bits[::-1])
            half = acc.shape[0] // 2
            parts[4 * m + node] = acc[:half]
            parts[4 * m + 2 + node] = swap(acc[half:], "pcol", 1)
    return unpack(parts)


def solution(mesh):
    return jax.shard_map(
        local,
        mesh=mesh,
        in_specs=(P("prow", "pcol"), P("prow", None, "pcol"), P()),
        out_specs=P(("pcol", "prow"), None, None),
        check_vma=False,
    )
```
